256 devices in a mesh: rep: 2 (over y_lo), exp: 128 (over y_hi, z, x, core).
Axes of the slice: x: 4, y: 4 (y_hi: 2, y_lo: 2; y = y_hi * 2 + y_lo), z: 8, core: 2. Of those that a mesh axis runs over, the one named last changes fastest.
Arguments:
- tokens: bfloat16 [32768, 2048], P(('rep', 'exp')), may hold values from -6 to 6
- out_grad: bfloat16 [32768, 2048], P(('rep', 'exp')), may hold values from -1.5 to 1.5
- route: int32 [32768, 4], P(('rep', 'exp')), may hold values from 0 to 127, as said below
- prob: bfloat16 [32768, 4], P(('rep', 'exp')), may hold values from 0.049804688 to 0.59765625
- w_gate: bfloat16 [128, 2048, 384], P('exp'), may hold values from -0.125 to 0.125
- w_up: bfloat16 [128, 2048, 384], P('exp'), may hold values from -0.125 to 0.125
- w_down: bfloat16 [128, 384, 2048], P('exp'), may hold values from -0.3125 to 0.3125
Outputs:
- grad_tokens: bfloat16 [32768, 2048], P(('rep', 'exp'))
- grad_prob: bfloat16 [32768, 4], P(('rep', 'exp'))
- grad_gate: bfloat16 [128, 2048, 384], P('exp', 'rep')
- grad_up: bfloat16 [128, 2048, 384], P('exp', 'rep')
- grad_down: bfloat16 [128, 384, 2048], P('exp', 'rep')
The draws below stay inside these ranges and needn't reach their ends.
Inputs may be any that keep to these rules, and one draw needn't show every extreme that they name: `route`: each row names 4 different experts. In each aligned block of 128 rows (the rows of one device) an expert is named by at most 8 rows; one expert, the same for all blocks, is named by exactly 8 rows of every block.
All inputs are finite; a program needn't handle non-finite values.
Results may differ from the reference program's by a relative error of at most 0.0059.
Values may be sent and summed in bfloat16 or wider, within the bound.
No kernel may reach another device: no remote copies, remote signals or barrier semaphores. Data moves between devices by JAX's collectives and lax.ppermute only.
A program may use at most 128 MiB of HBM per device.

```python
import jax
import jax.numpy as jnp
from jax import lax

D = 2048
F = 384
K = 4
TOK_DEV = 128
E = 128
TOKENS = 32768
CAP = 8
N_REP = 2


def draw_route(key, part):
    blocks = TOKENS // TOK_DEV
    rates = jax.random.randint(jax.random.fold_in(key, 11), (E,), 1, 17)
    favored = jax.random.randint(jax.random.fold_in(key, 12), (), 0, E)
    block_keys = jax.random.split(jax.random.fold_in(key, 13), blocks)
    labels = jnp.arange(E, dtype=jnp.int32)

    def one_block(block_key):
        keys = jax.random.split(block_key, 3)
        forced = jax.random.permutation(keys[0], TOK_DEV) < CAP
        noise = jax.random.randint(keys[1], (TOK_DEV, E), 0, 65536)
        shuffle = jax.random.randint(keys[2], (TOK_DEV, K), 0, 65536)

        def advance(counts, inputs):
            force_here, row_noise = inputs
            score = row_noise * rates * E + labels
            score = jnp.where(counts >= CAP, -1 - labels, score)
            score = jnp.where(labels == favored, jnp.where(force_here, 2 ** 30, -4 * E), score)
            picked = lax.top_k(score, K)[1].astype(jnp.int32)
            counts = counts + jnp.sum((picked[:, None] == labels[None, :]).astype(jnp.int32), axis=0)
            return (counts, picked)
        final_counts, picked = lax.scan(advance, jnp.zeros((E,), jnp.int32), (forced, noise))
        arrange = jnp.argsort(shuffle, axis=1, stable=True)
        return jnp.take_along_axis(picked, arrange, axis=1)
    return jax.vmap(one_block)(block_keys).reshape(TOKENS, K).astype(jnp.int32)


def steps_of(rng, extent, cuts, smallest, largest):
    def one(position, blocks):
        steps = jax.random.uniform(jax.random.fold_in(jax.random.fold_in(rng, 6), position), (blocks,), jnp.float32, smallest / len(cuts), largest / len(cuts))
        return jnp.repeat(jnp.exp(steps), extent[position] // blocks).reshape((-1,) + (1,) * (len(extent) - position - 1))

    level = one(*cuts[0])
    for cut in cuts[1:]:
        level = level * one(*cut)
    return level


def scatter_about(own_key, extent, spread, bound, cuts=(), kind=jnp.bfloat16):
    result = jax.random.normal(own_key, extent, jnp.float32) * spread
    if len(cuts) > 0:
        result = steps_of(own_key, extent, cuts, -0.22, 0.18) * result
    return jnp.clip(result, min=-bound, max=bound).astype(kind)


def setup_inputs(seed: int = 0) -> dict:
    arg_keys = jax.random.split(jax.random.key(seed), 8)
    tokens = scatter_about(arg_keys[0], (TOKENS, D), 1.0, 6.0, ((0, 256),))
    out_grad = scatter_about(arg_keys[1], (TOKENS, D), 0.25, 1.5, ((0, 256),))
    route = draw_route(jax.random.fold_in(arg_keys[7], 71), 0)
    prob = jnp.clip(0.049804688 + 0.54785156 * jax.random.uniform(arg_keys[3], (TOKENS, K), jnp.float32) ** steps_of(arg_keys[3], (TOKENS, K), ((0, 256),), -0.2, 0.2), 0.049804688, 0.59765625).astype(jnp.bfloat16)
    w_gate = scatter_about(arg_keys[4], (E, D, F), D ** -0.5, 0.125, ((0, 128),))
    w_up = scatter_about(arg_keys[5], (E, D, F), D ** -0.5, 0.125, ((0, 128),))
    w_down = scatter_about(arg_keys[6], (E, F, D), F ** -0.5, 0.3125, ((0, 128),))
    return dict(tokens=tokens, out_grad=out_grad, route=route, prob=prob, w_gate=w_gate, w_up=w_up, w_down=w_down)


def expert_pass(input_rows, row_gradients, rows_prob, gate_weight, up_weight, down_weight):
    gate_preactivation = jnp.dot(input_rows, gate_weight, preferred_element_type=jnp.float32)
    up_preactivation = jnp.dot(input_rows, up_weight, preferred_element_type=jnp.float32)
    backward_rows = jnp.dot(row_gradients, down_weight.T, preferred_element_type=jnp.float32)
    sigma = jax.nn.sigmoid(gate_preactivation)
    active = gate_preactivation * sigma
    hidden = active * up_preactivation
    grad_weight = jnp.sum(backward_rows * hidden, axis=-1).astype(jnp.bfloat16)
    weight = rows_prob.astype(jnp.float32)[:, None]
    scaled_output = (weight * hidden).astype(jnp.bfloat16)
    d_back = weight * backward_rows
    gate_gradient = (d_back * up_preactivation * sigma * (1.0 + gate_preactivation * (1.0 - sigma))).astype(jnp.bfloat16)
    up_gradient = (d_back * active).astype(jnp.bfloat16)
    contrib = jnp.dot(gate_gradient, gate_weight.T, preferred_element_type=jnp.float32)
    contrib = (contrib + jnp.dot(up_gradient, up_weight.T, preferred_element_type=jnp.float32)).astype(jnp.bfloat16)
    return contrib, grad_weight, scaled_output, gate_gradient, up_gradient


def group_sums(left, right, groups):
    total = jnp.zeros((left.shape[1], right.shape[1]), jnp.float32)
    for group in range(N_REP):
        inside = (groups == group)[:, None]
        masked = jnp.where(inside, left, jnp.zeros((), left.dtype))
        part = jnp.dot(masked.T, right, preferred_element_type=jnp.float32).astype(jnp.bfloat16)
        total = total + lax.optimization_barrier(part).astype(jnp.float32)
    return total.astype(jnp.bfloat16)


def reference(tokens, out_grad, route, prob, w_gate, w_up, w_down):
    flat = route.reshape(-1).astype(jnp.int32)
    labels = jnp.arange(E, dtype=jnp.int32)
    counts = jnp.sum((flat[:, None] == labels[None, :]).astype(jnp.int32), axis=0)
    starts = (jnp.cumsum(counts) - counts).astype(jnp.int32)
    most = (TOKENS // TOK_DEV) * CAP
    order = jnp.concatenate([jnp.argsort(flat, stable=True).astype(jnp.int32), jnp.zeros((most,), jnp.int32)])
    prob_flat = prob.reshape(-1)
    group_rows = TOKENS // N_REP

    def visit(carry, inputs):
        grad_acc, prob_acc = carry
        expert, gate_weight, up_weight, down_weight = inputs
        picks = lax.dynamic_slice_in_dim(order, starts[expert], most)
        valid = jnp.arange(most, dtype=jnp.int32) < counts[expert]
        rows = (picks // K).astype(jnp.int32)
        groups = (rows // group_rows).astype(jnp.int32)
        input_rows = jnp.where(valid[:, None], tokens[rows], jnp.zeros((), tokens.dtype))
        row_gradients = jnp.where(valid[:, None], out_grad[rows], jnp.zeros((), out_grad.dtype))
        rows_prob = jnp.where(valid, prob_flat[picks], jnp.zeros((), prob.dtype))
        contrib, grad_weight, scaled_output, gate_gradient, up_gradient = expert_pass(input_rows, row_gradients, rows_prob, gate_weight, up_weight, down_weight)
        grad_down = group_sums(scaled_output, row_gradients, groups)
        grad_gate = group_sums(input_rows, gate_gradient, groups)
        grad_up = group_sums(input_rows, up_gradient, groups)
        contrib = lax.optimization_barrier(contrib).astype(jnp.float32)
        grad_weight = lax.optimization_barrier(grad_weight).astype(jnp.float32)
        grad_acc = grad_acc.at[rows].add(jnp.where(valid[:, None], contrib, jnp.zeros((), jnp.float32)))
        prob_acc = prob_acc.at[picks].add(jnp.where(valid, grad_weight, jnp.zeros((), jnp.float32)))
        return (grad_acc, prob_acc), (grad_gate, grad_up, grad_down)

    start_state = (jnp.zeros((TOKENS, D), jnp.float32), jnp.zeros((TOKENS * K,), jnp.float32))
    finals, stacked = lax.scan(visit, start_state, (labels, w_gate, w_up, w_down))
    grad_acc, prob_acc = finals
    grad_gate, grad_up, grad_down = stacked
    return (grad_acc.astype(jnp.bfloat16), prob_acc.reshape(TOKENS, K).astype(jnp.bfloat16), grad_gate, grad_up, grad_down)
```

```python
import functools

import jax
import jax.numpy as jnp
from jax import lax
from jax.experimental import pallas as pl
from jax.experimental.pallas import tpu as pltpu
from jax.sharding import Mesh, PartitionSpec as P


YH, Z, X, C = 2, 8, 4, 2
PLANE = ("yh", "x", "c")
ALL = ("rep", "yh", "z", "x", "c")
PEERS = YH * X * C
CAP = 8
SLOTS = PEERS * CAP
LANES = 128
META = 8
FAR = Z // 2
ROUNDS = (("a0", "a1"), ("b1", "a2", "b2"), ("a3", "b3", "a4"))
BF, F32 = jnp.bfloat16, jnp.float32
SMEM = pl.BlockSpec(memory_space=pltpu.SMEM)
VMEM = pl.BlockSpec(memory_space=pltpu.VMEM)


def params(mib=63):
    return pltpu.CompilerParams(vmem_limit_bytes=mib * 1024 * 1024)


def z_shift(value, step, cross=False):
    pairs = []
    for i in range(Z):
        for core, move in enumerate((step, -step)):
            pairs.append((i * C + core, (i + move) % Z * C + (core ^ cross)))
    return lax.ppermute(value, ("z", "c"), pairs)


def swap(value, axis):
    return lax.ppermute(value, axis, [(0, 1), (1, 0)])


def pack_kernel(route_ref, prob_ref, tokens_ref, grad_ref, out_ref):
    rows, width = tokens_ref.shape
    topk = route_ref.shape[0]
    experts = YH * Z * X * C
    label = lax.broadcasted_iota(jnp.int32, (experts, rows), 0)
    hits = [label == route_ref[k : k + 1, :] for k in range(topk)]
    named = functools.reduce(jnp.logical_or, hits).astype(F32).astype(BF)
    before = lax.broadcasted_iota(jnp.int32, (rows, rows), 0) < lax.broadcasted_iota(
        jnp.int32, (rows, rows), 1
    )
    earlier = jnp.dot(named, before.astype(F32).astype(BF), preferred_element_type=F32)
    out_ref[0:rows, :] = tokens_ref[...]
    out_ref[rows : 2 * rows, :] = grad_ref[...]
    expert = route_ref[...]
    position = jnp.concatenate(
        [jnp.sum(jnp.where(h, earlier, 0.0), axis=0, keepdims=True) for h in hits], axis=0
    )
    per_half = Z * X * C
    slot = (expert // per_half) * (X * C * CAP) + (expert % (X * C)) * CAP
    slot = slot.astype(F32) + position
    plane = ((expert // (X * C)) % Z).astype(F32)
    meta = jnp.concatenate([slot, plane, prob_ref[...].astype(F32)], axis=1)
    meta = jnp.concatenate([meta, jnp.zeros((META - topk, 3 * rows), F32)], axis=0)
    meta = jnp.concatenate([meta, jnp.zeros((META, width - 3 * rows), F32)], axis=1)
    out_ref[2 * rows : 2 * rows + META, :] = meta.astype(BF)


def pack(route, prob, tokens, grad):
    rows, width = tokens.shape
    return pl.pallas_call(
        pack_kernel,
        out_shape=jax.ShapeDtypeStruct((2 * rows + META, width), BF),
        compiler_params=params(),
        name="pack",
    )(route.T, prob.T, tokens, grad)


def slot_hits(meta, z_me, topk):
    rows = LANES
    label = lax.broadcasted_iota(jnp.int32, (SLOTS, rows), 0).astype(F32)
    hits = []
    for k in range(topk):
        slot, plane = meta[k : k + 1, 0:rows], meta[k : k + 1, rows : 2 * rows]
        hits.append((label == slot) & (plane == z_me))
    return hits


def select_rows(meta, z_me, topk):
    hits = slot_hits(meta, z_me, topk)
    return hits, functools.reduce(jnp.logical_or, hits).astype(F32).astype(BF)


def build_kernel(topk, count, z_ref, *refs):
    out_ref = refs[-1]
    z_me = z_ref[0].astype(F32)
    for b in range(count):
        block = refs[b]
        width = block.shape[1]
        meta = block[2 * LANES : 2 * LANES + META, 0 : 3 * LANES].astype(F32)
        hits, select = select_rows(meta, z_me, topk)
        weight = sum(
            jnp.where(h, meta[k : k + 1, 2 * LANES : 3 * LANES], 0.0)
            for k, h in enumerate(hits)
        )
        weight = jnp.sum(weight, axis=1, keepdims=True)
        for part in range(2):
            rows = jnp.dot(
                select, block[part * LANES : (part + 1) * LANES, :], preferred_element_type=F32
            )
            out_ref[:, b, :, part * width : (part + 1) * width] = rows.reshape(
                PEERS, CAP, width
            ).astype(BF)
        out_ref[:, b, :, 2 * width :] = (
            jnp.broadcast_to(weight, (SLOTS, LANES)).reshape(PEERS, CAP, LANES).astype(BF)
        )


def build(z_me, blocks, topk):
    width = blocks[0].shape[1]
    count = len(blocks)
    return pl.pallas_call(
        functools.partial(build_kernel, topk, count),
        in_specs=[SMEM] + [VMEM] * count,
        out_shape=jax.ShapeDtypeStruct((PEERS, count, CAP, 2 * width + LANES), BF),
        compiler_params=params(),
        name="build",
    )(z_me, *blocks)


def expert_kernel(carried, rows_ref, wg_ref, wu_ref, wd_ref, *refs):
    back_ref, x_ref, sc_ref, dg_ref, du_ref = refs[carried:]
    width = wg_ref.shape[0]
    rows = rows_ref[...]
    x_ref[...] = rows[:, 0 : 2 * width]
    x, g = rows[:, 0:width], rows[:, width : 2 * width]
    weight = rows[:, 2 * width : 2 * width + 1].astype(F32)
    last = (((1,), (1,)), ((), ()))
    gate = jnp.dot(x, wg_ref[...], preferred_element_type=F32)
    up = jnp.dot(x, wu_ref[...], preferred_element_type=F32)
    back = lax.dot_general(g, wd_ref[...], last, preferred_element_type=F32)
    sigma = jax.nn.sigmoid(gate)
    active = gate * sigma
    hidden = active * up
    weight_grad = jnp.sum(back * hidden, axis=1, keepdims=True)
    sc_ref[...] = (weight * hidden).astype(BF)
    d_back = weight * back
    d_gate = (d_back * up * sigma * (1.0 + gate * (1.0 - sigma))).astype(BF)
    d_up = (d_back * active).astype(BF)
    dg_ref[...] = d_gate
    du_ref[...] = d_up
    contrib = lax.dot_general(d_gate, wg_ref[...], last, preferred_element_type=F32)
    contrib += lax.dot_general(d_up, wu_ref[...], last, preferred_element_type=F32)
    peers, count, cap, _ = back_ref.shape
    back_ref[:, :, :, 0:width] = contrib.reshape(peers, count, cap, width).astype(BF)
    weight_grad = jnp.broadcast_to(weight_grad, (rows.shape[0], LANES))
    back_ref[:, :, :, width:] = weight_grad.reshape(peers, count, cap, LANES).astype(BF)


def expert(rows, wg, wu, wd, kept, start, total):
    width, hidden = wg.shape
    count = rows.shape[0]
    full = lambda a: pl.BlockSpec(a.shape, lambda i: (0, 0))
    rows_at = lambda n: pl.BlockSpec((count, n), lambda i: (start // count, 0))
    kept_widths = (2 * width, hidden, hidden, hidden)
    back_shape = (PEERS, count // SLOTS, CAP, width + LANES)
    return pl.pallas_call(
        functools.partial(expert_kernel, len(kept)),
        grid=(1,),
        in_specs=[full(rows), full(wg), full(wu), full(wd)]
        + [pl.BlockSpec(memory_space=pl.ANY)] * len(kept),
        out_specs=[pl.BlockSpec(back_shape, lambda i: (0, 0, 0, 0))]
        + [rows_at(n) for n in kept_widths],
        out_shape=[jax.ShapeDtypeStruct(back_shape, BF)]
        + [jax.ShapeDtypeStruct((total, n), BF) for n in kept_widths],
        input_output_aliases={4 + i: 1 + i for i in range(len(kept))},
        compiler_params=params(),
        name="expert",
    )(rows, wg, wu, wd, *kept)


def weights_kernel(rep_ref, x_ref, g_ref, sc_ref, dg_ref, du_ref, *refs):
    keep_g, send_g, keep_u, send_u, keep_d, send_d, down_acc = refs
    step, half_steps = pl.program_id(0), pl.num_programs(0) // 2
    first = (((0,), (0,)), ((), ()))
    x = x_ref[...]
    gate = lax.dot_general(x, dg_ref[...], first, preferred_element_type=F32).astype(BF)
    up = lax.dot_general(x, du_ref[...], first, preferred_element_type=F32).astype(BF)

    @pl.when(step < half_steps)
    def _():
        send_g[...] = gate
        send_u[...] = up

    @pl.when(step >= half_steps)
    def _():
        keep_g[...] = gate
        keep_u[...] = up

    down_acc[...] = lax.dot_general(
        sc_ref[...], g_ref[...], first, preferred_element_type=F32
    )
    half = keep_d.shape[0]
    rep = rep_ref[0]
    keep_d[...] = down_acc[pl.ds(pl.multiple_of(rep * half, half), half), :].astype(BF)
    send_d[...] = down_acc[pl.ds(pl.multiple_of((1 - rep) * half, half), half), :].astype(BF)


def weights(rep, rows, sc, dg, du):
    total, hidden = sc.shape
    width = rows.shape[1] // 2
    tile = 512
    steps = width // tile
    half = steps // 2

    def chosen(i, rep):
        return lax.rem(i + (1 - rep[0]) * half, steps)

    whole = pl.BlockSpec((total, hidden), lambda i, rep: (0, 0), pipeline_mode=pl.Buffered(1))
    keep = pl.BlockSpec((tile, hidden), lambda i, rep: (jnp.maximum(i - half, 0), 0))
    send = pl.BlockSpec((tile, hidden), lambda i, rep: (jnp.minimum(i, half - 1), 0))
    down = pl.BlockSpec((hidden // 2, tile), lambda i, rep: (0, i))
    gu_shape = jax.ShapeDtypeStruct((width // 2, hidden), BF)
    down_shape = jax.ShapeDtypeStruct((hidden // 2, width), BF)
    return pl.pallas_call(
        weights_kernel,
        grid_spec=pltpu.PrefetchScalarGridSpec(
            num_scalar_prefetch=1,
            grid=(steps,),
            in_specs=[
                pl.BlockSpec((total, tile), lambda i, rep: (0, chosen(i, rep))),
                pl.BlockSpec((total, tile), lambda i, rep: (0, steps + i)),
                whole,
                whole,
                whole,
            ],
            out_specs=[keep, send, keep, send, down, down],
            scratch_shapes=[pltpu.VMEM((hidden, tile), F32)],
        ),
        out_shape=[gu_shape] * 4 + [down_shape] * 2,
        compiler_params=params(),
        name="weights",
    )(rep, rows, rows, sc, dg, du)


def combine_kernel(topk, count, z_ref, back_ref, *refs):
    z_me = z_ref[0].astype(F32)
    for b in range(count):
        meta = refs[b][:, 0 : 3 * LANES].astype(F32)
        out_ref = refs[count + b]
        width = out_ref.shape[1]
        hits, select = select_rows(meta, z_me, topk)
        rows = back_ref[:, b, :, 0:width].astype(F32).reshape(SLOTS, width).astype(BF)
        part = lax.dot_general(
            select, rows, (((0,), (0,)), ((), ())), preferred_element_type=F32
        )
        out_ref[0:LANES, :] = part.astype(out_ref.dtype)
        value = back_ref[:, b, :, width:].astype(F32).reshape(SLOTS, LANES)
        grads = [jnp.sum(jnp.where(h, value, 0.0), axis=0, keepdims=True) for h in hits]
        grads.append(jnp.zeros((META - topk, LANES), F32))
        grads = jnp.concatenate(grads, axis=0)
        grads = jnp.concatenate([grads, jnp.zeros((META, width - LANES), F32)], axis=1)
        out_ref[LANES : LANES + META, :] = grads.astype(out_ref.dtype)


def combine(z_me, back, blocks, topk, kinds):
    width = back.shape[-1] - LANES
    count = len(blocks)
    last = blocks[0].shape[0] // META - 1
    return pl.pallas_call(
        functools.partial(combine_kernel, topk, count),
        grid=(1,),
        in_specs=[SMEM, pl.BlockSpec(back.shape, lambda i: (0, 0, 0, 0))]
        + [pl.BlockSpec((META, width), lambda i: (last, 0))] * count,
        out_specs=[pl.BlockSpec((LANES + META, width), lambda i: (0, 0))] * count,
        out_shape=[jax.ShapeDtypeStruct((LANES + META, width), k) for k in kinds],
        compiler_params=params(),
        name="combine",
    )(z_me, back, *blocks)


def plane_exchange(value):
    return lax.all_to_all(value, PLANE, split_axis=0, concat_axis=0, tiled=True)


def body(tokens, out_grad, route, prob, w_gate, w_up, w_down):
    local, _ = tokens.shape
    topk = route.shape[1]
    wg, wu, wd = w_gate[0], w_up[0], w_down[0]
    z_me = lax.axis_index("z").reshape(1)
    rep = lax.axis_index("rep").reshape(1)

    blocks = {"a0": pack(route, prob, tokens, out_grad)}
    blocks["a1"] = z_shift(blocks["a0"], 1)
    blocks["b0"] = swap(blocks["a0"], "c")
    for s in range(1, FAR + 1):
        for kind in "ab":
            name = f"{kind}{s}"
            if name not in blocks and name != f"b{FAR}":
                blocks[name] = z_shift(blocks[f"{kind}{s - 1}"], 1)

    kept, backs = [], []
    starts = (6 * SLOTS, 3 * SLOTS, 0)
    for i, group in enumerate(ROUNDS):
        sent = build(z_me, [blocks[r] for r in group], topk)
        rows = plane_exchange(sent)
        rows = rows.reshape(-1, rows.shape[-1])
        back, *kept = expert(rows, wg, wu, wd, kept, starts[i], Z * SLOTS)
        backs.append(back)
    halves = weights(rep, *kept)
    grads = []
    for name, keep, send in zip(("gate", "up", "down"), halves[0::2], halves[1::2]):
        got = swap(send, "rep")
        grads.append((keep.astype(F32) + got.astype(F32)).astype(BF)[None])

    partial = {}
    for i in range(len(ROUNDS) - 1, -1, -1):
        returned = plane_exchange(backs[i])
        group = ROUNDS[i]
        kinds = [F32 if r == "a0" else BF for r in group]
        parts = combine(z_me, returned, [blocks[r] for r in group], topk, kinds)
        partial.update(zip(group, parts))
    moving = {"a": partial[f"a{FAR}"], "b": partial[f"b{FAR - 1}"]}
    for s in range(FAR - 1, -1, -1):
        for kind in "ab":
            if f"{kind}{s}" == f"b{FAR - 1}":
                continue
            came = z_shift(moving[kind], -1, cross=kind + str(s) == "b0")
            if s > 0:
                came = (partial[f"{kind}{s}"].astype(F32) + came.astype(F32)).astype(BF)
            moving[kind] = came
    ends = (partial["a0"], moving["a"], moving["b"])
    grad_tokens = sum(e[:local].astype(F32) for e in ends).astype(BF)
    grad_prob = sum(e[local : local + topk, :local].astype(F32) for e in ends).T.astype(BF)
    return (grad_tokens, grad_prob, *grads)


def solution(mesh):
    fine = Mesh(mesh.devices.reshape(-1, YH, Z, X, C), ALL)
    exp = ("yh", "z", "x", "c")
    placed = (P(ALL, None),) * 4 + (P(exp, None, None),) * 3
    return jax.shard_map(
        body,
        mesh=fine,
        in_specs=placed,
        out_specs=(P(ALL, None),) * 2 + (P(exp, "rep", None),) * 3,
        check_vma=False,
    )
```

```python
import functools

import jax
import jax.numpy as jnp
from jax import lax
from jax.experimental import pallas as pl
from jax.experimental.pallas import tpu as pltpu
from jax.sharding import Mesh, PartitionSpec as P


YH, Z, X, C = 2, 8, 4, 2
PLANE = ("yh", "x", "c")
ALL = ("rep", "yh", "z", "x", "c")
PEERS = YH * X * C
CAP = 8
SLOTS = PEERS * CAP
LANES = 128
META = 8
FAR = Z // 2
ROUNDS = (
    (("a0", "a1"), 6, ((0, 0, 1), (1, 3, 1))),
    (("b1", "a2", "b2"), 3, ((1, 0, 3),)),
    (("a3", "b3", "a4"), 0, ((2, 0, 3),)),
)
RETURNS = (("a0",), ("b1", "a2", "b2", "a1"), ("a3", "b3", "a4"))
BF, F32 = jnp.bfloat16, jnp.float32
SMEM = pl.BlockSpec(memory_space=pltpu.SMEM)
VMEM = pl.BlockSpec(memory_space=pltpu.VMEM)


def params(mib=63):
    return pltpu.CompilerParams(vmem_limit_bytes=mib * 1024 * 1024)


def z_shift(value, step, cross=False):
    pairs = []
    for i in range(Z):
        for core, move in enumerate((step, -step)):
            pairs.append((i * C + core, (i + move) % Z * C + (core ^ cross)))
    return lax.ppermute(value, ("z", "c"), pairs)


def swap(value, axis):
    return lax.ppermute(value, axis, [(0, 1), (1, 0)])


def pack_kernel(route_ref, prob_ref, tokens_ref, grad_ref, out_ref):
    rows, width = tokens_ref.shape
    topk = route_ref.shape[0]
    experts = YH * Z * X * C
    label = lax.broadcasted_iota(jnp.int32, (experts, rows), 0)
    hits = [label == route_ref[k : k + 1, :] for k in range(topk)]
    named = functools.reduce(jnp.logical_or, hits).astype(F32).astype(BF)
    before = lax.broadcasted_iota(jnp.int32, (rows, rows), 0) < lax.broadcasted_iota(
        jnp.int32, (rows, rows), 1
    )
    earlier = jnp.dot(named, before.astype(F32).astype(BF), preferred_element_type=F32)
    out_ref[0:rows, :] = tokens_ref[...]
    out_ref[rows : 2 * rows, :] = grad_ref[...]
    expert = route_ref[...]
    position = jnp.concatenate(
        [jnp.sum(jnp.where(h, earlier, 0.0), axis=0, keepdims=True) for h in hits], axis=0
    )
    per_half = Z * X * C
    slot = (expert // per_half) * (X * C * CAP) + (expert % (X * C)) * CAP
    slot = slot.astype(F32) + position
    plane = ((expert // (X * C)) % Z).astype(F32)
    meta = jnp.concatenate([slot, plane, prob_ref[...].astype(F32)], axis=1)
    meta = jnp.concatenate([meta, jnp.zeros((META - topk, 3 * rows), F32)], axis=0)
    meta = jnp.concatenate([meta, jnp.zeros((META, width - 3 * rows), F32)], axis=1)
    out_ref[2 * rows : 2 * rows + META, :] = meta.astype(BF)


def pack(route, prob, tokens, grad):
    rows, width = tokens.shape
    return pl.pallas_call(
        pack_kernel,
        out_shape=jax.ShapeDtypeStruct((2 * rows + META, width), BF),
        compiler_params=params(),
        name="pack",
    )(route.T, prob.T, tokens, grad)


def slot_hits(meta, z_me, topk):
    rows = LANES
    label = lax.broadcasted_iota(jnp.int32, (SLOTS, rows), 0).astype(F32)
    hits = []
    for k in range(topk):
        slot, plane = meta[k : k + 1, 0:rows], meta[k : k + 1, rows : 2 * rows]
        hits.append((label == slot) & (plane == z_me))
    return hits


def select_rows(meta, z_me, topk):
    hits = slot_hits(meta, z_me, topk)
    return hits, functools.reduce(jnp.logical_or, hits).astype(F32).astype(BF)


def build_kernel(topk, count, z_ref, *refs):
    out_ref = refs[-1]
    z_me = z_ref[0].astype(F32)
    for b in range(count):
        block = refs[b]
        width = block.shape[1]
        meta = block[2 * LANES : 2 * LANES + META, 0 : 3 * LANES].astype(F32)
        hits, select = select_rows(meta, z_me, topk)
        weight = sum(
            jnp.where(h, meta[k : k + 1, 2 * LANES : 3 * LANES], 0.0)
            for k, h in enumerate(hits)
        )
        weight = jnp.sum(weight, axis=1, keepdims=True)
        for part in range(2):
            rows = jnp.dot(
                select, block[part * LANES : (part + 1) * LANES, :], preferred_element_type=F32
            )
            if part == 1:
                rows *= weight
            out_ref[:, b, :, part * width : (part + 1) * width] = rows.reshape(
                PEERS, CAP, width
            ).astype(BF)


def build(z_me, blocks, topk):
    width = blocks[0].shape[1]
    count = len(blocks)
    return pl.pallas_call(
        functools.partial(build_kernel, topk, count),
        in_specs=[SMEM] + [VMEM] * count,
        out_shape=jax.ShapeDtypeStruct((PEERS, count, CAP, 2 * width), BF),
        compiler_params=params(),
        name="build",
    )(z_me, *blocks)


def expert_kernel(carried, rows_ref, wg_ref, wu_ref, wd_ref, *refs):
    *back_refs, x_ref, sc_ref, dg_ref, du_ref = refs[carried:]
    width = wg_ref.shape[0]
    rows = rows_ref[...]
    x_ref[...] = rows
    x, g = rows[:, 0:width], rows[:, width:]
    last = (((1,), (1,)), ((), ()))
    gate = jnp.dot(x, wg_ref[...], preferred_element_type=F32)
    up = jnp.dot(x, wu_ref[...], preferred_element_type=F32)
    back = lax.dot_general(g, wd_ref[...], last, preferred_element_type=F32)
    sigma = jax.nn.sigmoid(gate)
    active = gate * sigma
    hidden = active * up
    weight_grad = jnp.sum(back * hidden, axis=1, keepdims=True)
    sc_ref[...] = hidden.astype(BF)
    d_gate = (back * up * sigma * (1.0 + gate * (1.0 - sigma))).astype(BF)
    d_up = (back * active).astype(BF)
    dg_ref[...] = d_gate
    du_ref[...] = d_up
    contrib = lax.dot_general(d_gate, wg_ref[...], last, preferred_element_type=F32)
    contrib += lax.dot_general(d_up, wu_ref[...], last, preferred_element_type=F32)
    blocks = rows.shape[0] // SLOTS
    contrib = contrib.reshape(PEERS, blocks, CAP, width)
    weight_grad = jnp.broadcast_to(weight_grad, (rows.shape[0], LANES))
    weight_grad = weight_grad.reshape(PEERS, blocks, CAP, LANES)
    at = 0
    for ref in back_refs:
        n = ref.shape[1]
        ref[:, :, :, 0:width] = contrib[:, at : at + n].astype(BF)
        ref[:, :, :, width:] = weight_grad[:, at : at + n].astype(BF)
        at += n


def expert(rows, wg, wu, wd, kept, start, backs, targets):
    width, hidden = wg.shape
    count = rows.shape[0]
    full = lambda a: pl.BlockSpec(a.shape, lambda i: (0, 0))
    rows_at = lambda n: pl.BlockSpec((count, n), lambda i: (start * SLOTS // count, 0))

    def back_spec(n, place):
        return pl.BlockSpec((PEERS, n, CAP, width + LANES), lambda i: (0, place // n, 0, 0))

    kept_widths = (2 * width, hidden, hidden, hidden)
    carried = [(backs[w], o) for o, (w, _, _) in enumerate(targets) if w in backs]
    carried += [(k, len(targets) + i) for i, k in enumerate(kept)]
    return pl.pallas_call(
        functools.partial(expert_kernel, len(carried)),
        grid=(1,),
        in_specs=[full(rows), full(wg), full(wu), full(wd)]
        + [pl.BlockSpec(memory_space=pl.ANY)] * len(carried),
        out_specs=[back_spec(n, place) for _, place, n in targets]
        + [rows_at(n) for n in kept_widths],
        out_shape=[
            jax.ShapeDtypeStruct((PEERS, len(RETURNS[w]), CAP, width + LANES), BF)
            for w, _, _ in targets
        ]
        + [jax.ShapeDtypeStruct((Z * SLOTS, n), BF) for n in kept_widths],
        input_output_aliases={4 + i: o for i, (_, o) in enumerate(carried)},
        compiler_params=params(),
        name="expert",
    )(rows, wg, wu, wd, *[a for a, _ in carried])


FIRST = (((0,), (0,)), ((), ()))


def down_kernel(rep_ref, g_ref, sc_ref, keep_ref, send_ref, acc_ref):
    acc_ref[...] = lax.dot_general(sc_ref[...], g_ref[...], FIRST, preferred_element_type=F32)
    half, rep = keep_ref.shape[0], rep_ref[0]
    keep_ref[...] = acc_ref[pl.ds(pl.multiple_of(rep * half, half), half), :].astype(BF)
    send_ref[...] = acc_ref[pl.ds(pl.multiple_of((1 - rep) * half, half), half), :].astype(BF)


def gate_up_kernel(rep_ref, x_ref, dg_ref, du_ref, *outs):
    keep_g, send_g, keep_u, send_u = outs
    step, half_steps = pl.program_id(0), pl.num_programs(0) // 2
    x = x_ref[...]
    gate = lax.dot_general(x, dg_ref[...], FIRST, preferred_element_type=F32).astype(BF)
    up = lax.dot_general(x, du_ref[...], FIRST, preferred_element_type=F32).astype(BF)

    @pl.when(step < half_steps)
    def _():
        send_g[...] = gate
        send_u[...] = up

    @pl.when(step >= half_steps)
    def _():
        keep_g[...] = gate
        keep_u[...] = up


def weights_down(rep, rows, sc):
    total, hidden = sc.shape
    width = rows.shape[1] // 2
    tile = 512
    steps = width // tile
    down = pl.BlockSpec((hidden // 2, tile), lambda i, rep: (0, i))
    return pl.pallas_call(
        down_kernel,
        grid_spec=pltpu.PrefetchScalarGridSpec(
            num_scalar_prefetch=1,
            grid=(steps,),
            in_specs=[
                pl.BlockSpec((total, tile), lambda i, rep: (0, steps + i)),
                pl.BlockSpec((total, hidden), lambda i, rep: (0, 0)),
            ],
            out_specs=[down, down],
            scratch_shapes=[pltpu.VMEM((hidden, tile), F32)],
        ),
        out_shape=[jax.ShapeDtypeStruct((hidden // 2, width), BF)] * 2,
        compiler_params=params(),
        name="weights_down",
    )(rep, rows, sc)


def weights_gate_up(rep, rows, dg, du):
    total, hidden = dg.shape
    width = rows.shape[1] // 2
    tile = 512
    steps = width // tile
    half = steps // 2
    whole = pl.BlockSpec((total, hidden), lambda i, rep: (0, 0))
    keep = pl.BlockSpec((tile, hidden), lambda i, rep: (jnp.maximum(i - half, 0), 0))
    send = pl.BlockSpec((tile, hidden), lambda i, rep: (jnp.minimum(i, half - 1), 0))
    return pl.pallas_call(
        gate_up_kernel,
        grid_spec=pltpu.PrefetchScalarGridSpec(
            num_scalar_prefetch=1,
            grid=(steps,),
            in_specs=[
                pl.BlockSpec(
                    (total, tile), lambda i, rep: (0, lax.rem(i + (1 - rep[0]) * half, steps))
                ),
                whole,
                whole,
            ],
            out_specs=[keep, send, keep, send],
        ),
        out_shape=[jax.ShapeDtypeStruct((width // 2, hidden), BF)] * 4,
        compiler_params=params(),
        name="weights_gate_up",
    )(rep, rows, dg, du)


def combine_kernel(topk, count, z_ref, back_ref, *refs):
    z_me = z_ref[0].astype(F32)
    for b in range(count):
        meta = refs[b][:, 0 : 3 * LANES].astype(F32)
        out_ref = refs[count + b]
        width = out_ref.shape[1]
        hits, select = select_rows(meta, z_me, topk)
        rows = back_ref[:, b, :, 0:width].astype(F32).reshape(SLOTS, width).astype(BF)
        part = lax.dot_general(
            select, rows, (((0,), (0,)), ((), ())), preferred_element_type=F32
        )
        out_ref[0:LANES, :] = part.astype(out_ref.dtype)
        value = back_ref[:, b, :, width:].astype(F32).reshape(SLOTS, LANES)
        grads = [
            jnp.sum(jnp.where(h, value, 0.0), axis=0, keepdims=True)
            / meta[k : k + 1, 2 * LANES :]
            for k, h in enumerate(hits)
        ]
        grads.append(jnp.zeros((META - topk, LANES), F32))
        grads = jnp.concatenate(grads, axis=0)
        grads = jnp.concatenate([grads, jnp.zeros((META, width - LANES), F32)], axis=1)
        out_ref[LANES : LANES + META, :] = grads.astype(out_ref.dtype)


def combine(z_me, back, blocks, topk, kinds):
    width = back.shape[-1] - LANES
    count = len(blocks)
    last = blocks[0].shape[0] // META - 1
    return pl.pallas_call(
        functools.partial(combine_kernel, topk, count),
        grid=(1,),
        in_specs=[SMEM, pl.BlockSpec(back.shape, lambda i: (0, 0, 0, 0))]
        + [pl.BlockSpec((META, width), lambda i: (last, 0))] * count,
        out_specs=[pl.BlockSpec((LANES + META, width), lambda i: (0, 0))] * count,
        out_shape=[jax.ShapeDtypeStruct((LANES + META, width), k) for k in kinds],
        compiler_params=params(),
        name="combine",
    )(z_me, back, *blocks)


def plane_exchange(value):
    return lax.all_to_all(value, PLANE, split_axis=0, concat_axis=0, tiled=True)


def body(tokens, out_grad, route, prob, w_gate, w_up, w_down):
    local, _ = tokens.shape
    topk = route.shape[1]
    wg, wu, wd = w_gate[0], w_up[0], w_down[0]
    z_me = lax.axis_index("z").reshape(1)
    rep = lax.axis_index("rep").reshape(1)

    blocks = {"a0": pack(route, prob, tokens, out_grad)}
    blocks["a1"] = z_shift(blocks["a0"], 1)
    blocks["b0"] = swap(blocks["a0"], "c")
    for s in range(1, FAR + 1):
        for kind in "ab":
            name = f"{kind}{s}"
            if name not in blocks and name != f"b{FAR}":
                blocks[name] = z_shift(blocks[f"{kind}{s - 1}"], 1)

    kept, backs = [], {}
    for group, start, targets in ROUNDS:
        sent = build(z_me, [blocks[r] for r in group], topk)
        rows = plane_exchange(sent)
        rows = rows.reshape(-1, rows.shape[-1])
        done = expert(rows, wg, wu, wd, kept, start, backs, targets)
        kept = done[len(targets) :]
        backs.update(zip((w for w, _, _ in targets), done))
    rows, sc, dg, du = kept
    halves = weights_down(rep, rows, sc)
    halves = (*weights_gate_up(rep, rows, dg, du), *halves)
    grads = []
    for name, keep, send in zip(("gate", "up", "down"), halves[0::2], halves[1::2]):
        got = swap(send, "rep")
        grads.append((keep.astype(F32) + got.astype(F32)).astype(BF)[None])

    partial = {}
    for i, group in enumerate(RETURNS):
        returned = plane_exchange(backs[i])
        kinds = [F32 if r == "a0" else BF for r in group]
        parts = combine(z_me, returned, [blocks[r] for r in group], topk, kinds)
        partial.update(zip(group, parts))
    moving = {"a": partial[f"a{FAR}"], "b": partial[f"b{FAR - 1}"]}
    for s in range(FAR - 1, -1, -1):
        for kind in "ab":
            if f"{kind}{s}" == f"b{FAR - 1}":
                continue
            came = z_shift(moving[kind], -1, cross=kind + str(s) == "b0")
            if s > 0:
                came = (partial[f"{kind}{s}"].astype(F32) + came.astype(F32)).astype(BF)
            moving[kind] = came
    ends = (partial["a0"], moving["a"], moving["b"])
    grad_tokens = sum(e[:local].astype(F32) for e in ends).astype(BF)
    grad_prob = sum(e[local : local + topk, :local].astype(F32) for e in ends).T.astype(BF)
    return (grad_tokens, grad_prob, *grads)


def solution(mesh):
    fine = Mesh(mesh.devices.reshape(-1, YH, Z, X, C), ALL)
    exp = ("yh", "z", "x", "c")
    placed = (P(ALL, None),) * 4 + (P(exp, None, None),) * 3
    return jax.shard_map(
        body,
        mesh=fine,
        in_specs=placed,
        out_specs=(P(ALL, None),) * 2 + (P(exp, "rep", None),) * 3,
        check_vma=False,
    )
```

```python
import functools

import jax
import jax.numpy as jnp
from jax import lax
from jax.experimental import pallas as pl
from jax.experimental.pallas import tpu as pltpu
from jax.sharding import Mesh, PartitionSpec as P


YH, Z, X, C = 2, 8, 4, 2
PLANE = ("yh", "x", "c")
ALL = ("rep", "yh", "z", "x", "c")
PEERS = YH * X * C
CAP = 8
SLOTS = PEERS * CAP
LANES = 128
META = 8
FAR = Z // 2
ROUNDS = (
    (("a0", "a1"), 6, ((0, 0, 1), (1, 3, 1))),
    (("b1", "a2", "b2"), 3, ((1, 0, 3),)),
    (("a3", "b3", "a4"), 0, ((2, 0, 3),)),
)
RETURNS = (("a0",), ("b1", "a2", "b2", "a1"), ("a3", "b3", "a4"))
BF, F32 = jnp.bfloat16, jnp.float32
SMEM = pl.BlockSpec(memory_space=pltpu.SMEM)
VMEM = pl.BlockSpec(memory_space=pltpu.VMEM)


def params(mib=63):
    return pltpu.CompilerParams(vmem_limit_bytes=mib * 1024 * 1024)


def z_shift(value, step, cross=False):
    pairs = []
    for i in range(Z):
        for core, move in enumerate((step, -step)):
            pairs.append((i * C + core, (i + move) % Z * C + (core ^ cross)))
    return lax.ppermute(value, ("z", "c"), pairs)


def swap(value, axis):
    return lax.ppermute(value, axis, [(0, 1), (1, 0)])


def pack_kernel(route_ref, prob_ref, tokens_ref, grad_ref, out_ref):
    rows, width = tokens_ref.shape
    topk = route_ref.shape[0]
    experts = YH * Z * X * C
    label = lax.broadcasted_iota(jnp.int32, (experts, rows), 0)
    hits = [label == route_ref[k : k + 1, :] for k in range(topk)]
    named = functools.reduce(jnp.logical_or, hits).astype(F32).astype(BF)
    before = lax.broadcasted_iota(jnp.int32, (rows, rows), 0) < lax.broadcasted_iota(
        jnp.int32, (rows, rows), 1
    )
    earlier = jnp.dot(named, before.astype(F32).astype(BF), preferred_element_type=F32)
    out_ref[0:rows, :] = tokens_ref[...]
    out_ref[rows : 2 * rows, :] = grad_ref[...]
    expert = route_ref[...]
    position = jnp.concatenate(
        [jnp.sum(jnp.where(h, earlier, 0.0), axis=0, keepdims=True) for h in hits], axis=0
    )
    per_half = Z * X * C
    slot = (expert // per_half) * (X * C * CAP) + (expert % (X * C)) * CAP
    slot = slot.astype(F32) + position
    plane = ((expert // (X * C)) % Z).astype(F32)
    meta = jnp.concatenate([slot, plane, prob_ref[...].astype(F32)], axis=1)
    meta = jnp.concatenate([meta, jnp.zeros((META - topk, 3 * rows), F32)], axis=0)
    meta = jnp.concatenate([meta, jnp.zeros((META, width - 3 * rows), F32)], axis=1)
    out_ref[2 * rows : 2 * rows + META, :] = meta.astype(BF)


def pack(route, prob, tokens, grad):
    rows, width = tokens.shape
    return pl.pallas_call(
        pack_kernel,
        out_shape=jax.ShapeDtypeStruct((2 * rows + META, width), BF),
        compiler_params=params(),
        name="pack",
    )(route.T, prob.T, tokens, grad)


def slot_hits(meta, z_me, topk):
    rows = LANES
    label = lax.broadcasted_iota(jnp.int32, (SLOTS, rows), 0).astype(F32)
    hits = []
    for k in range(topk):
        slot, plane = meta[k : k + 1, 0:rows], meta[k : k + 1, rows : 2 * rows]
        hits.append((label == slot) & (plane == z_me))
    return hits


def select_rows(meta, z_me, topk):
    hits = slot_hits(meta, z_me, topk)
    return hits, functools.reduce(jnp.logical_or, hits).astype(F32).astype(BF)


def build_kernel(topk, count, z_ref, *refs):
    out_ref = refs[-1]
    z_me = z_ref[0].astype(F32)
    for b in range(count):
        block = refs[b]
        width = block.shape[1]
        meta = block[2 * LANES : 2 * LANES + META, 0 : 3 * LANES].astype(F32)
        hits, select = select_rows(meta, z_me, topk)
        weight = sum(
            jnp.where(h, meta[k : k + 1, 2 * LANES : 3 * LANES], 0.0)
            for k, h in enumerate(hits)
        )
        weight = jnp.sum(weight, axis=1, keepdims=True)
        for part in range(2):
            rows = jnp.dot(
                select, block[part * LANES : (part + 1) * LANES, :], preferred_element_type=F32
            )
            out_ref[:, b, :, part * width : (part + 1) * width] = rows.reshape(
                PEERS, CAP, width
            ).astype(BF)
        out_ref[:, b, :, 2 * width :] = (
            jnp.broadcast_to(weight, (SLOTS, LANES)).reshape(PEERS, CAP, LANES).astype(BF)
        )


def build(z_me, blocks, topk):
    width = blocks[0].shape[1]
    count = len(blocks)
    return pl.pallas_call(
        functools.partial(build_kernel, topk, count),
        in_specs=[SMEM] + [VMEM] * count,
        out_shape=jax.ShapeDtypeStruct((PEERS, count, CAP, 2 * width + LANES), BF),
        compiler_params=params(),
        name="build",
    )(z_me, *blocks)


def expert_kernel(carried, rows_ref, wg_ref, wu_ref, wd_ref, *refs):
    *back_refs, x_ref, sc_ref, dg_ref, du_ref = refs[carried:]
    width = wg_ref.shape[0]
    rows = rows_ref[...]
    x_ref[...] = rows[:, 0 : 2 * width]
    x, g = rows[:, 0:width], rows[:, width : 2 * width]
    weight = rows[:, 2 * width : 2 * width + 1].astype(F32)
    last = (((1,), (1,)), ((), ()))
    gate = jnp.dot(x, wg_ref[...], preferred_element_type=F32)
    up = jnp.dot(x, wu_ref[...], preferred_element_type=F32)
    back = lax.dot_general(g, wd_ref[...], last, preferred_element_type=F32)
    sigma = jax.nn.sigmoid(gate)
    active = gate * sigma
    hidden = active * up
    weight_grad = jnp.sum(back * hidden, axis=1, keepdims=True)
    sc_ref[...] = (weight * hidden).astype(BF)
    d_back = weight * back
    d_gate = (d_back * up * sigma * (1.0 + gate * (1.0 - sigma))).astype(BF)
    d_up = (d_back * active).astype(BF)
    dg_ref[...] = d_gate
    du_ref[...] = d_up
    contrib = lax.dot_general(d_gate, wg_ref[...], last, preferred_element_type=F32)
    contrib += lax.dot_general(d_up, wu_ref[...], last, preferred_element_type=F32)
    blocks = rows.shape[0] // SLOTS
    contrib = contrib.reshape(PEERS, blocks, CAP, width)
    weight_grad = jnp.broadcast_to(weight_grad, (rows.shape[0], LANES))
    weight_grad = weight_grad.reshape(PEERS, blocks, CAP, LANES)
    at = 0
    for ref in back_refs:
        n = ref.shape[1]
        ref[:, :, :, 0:width] = contrib[:, at : at + n].astype(BF)
        ref[:, :, :, width:] = weight_grad[:, at : at + n].astype(BF)
        at += n


def expert(rows, wg, wu, wd, kept, start, backs, targets):
    width, hidden = wg.shape
    count = rows.shape[0]
    full = lambda a: pl.BlockSpec(a.shape, lambda i: (0, 0))
    rows_at = lambda n: pl.BlockSpec((count, n), lambda i: (start * SLOTS // count, 0))

    def back_spec(n, place):
        return pl.BlockSpec((PEERS, n, CAP, width + LANES), lambda i: (0, place // n, 0, 0))

    kept_widths = (2 * width, hidden, hidden, hidden)
    carried = [(backs[w], o) for o, (w, _, _) in enumerate(targets) if w in backs]
    carried += [(k, len(targets) + i) for i, k in enumerate(kept)]
    return pl.pallas_call(
        functools.partial(expert_kernel, len(carried)),
        grid=(1,),
        in_specs=[full(rows), full(wg), full(wu), full(wd)]
        + [pl.BlockSpec(memory_space=pl.ANY)] * len(carried),
        out_specs=[back_spec(n, place) for _, place, n in targets]
        + [rows_at(n) for n in kept_widths],
        out_shape=[
            jax.ShapeDtypeStruct((PEERS, len(RETURNS[w]), CAP, width + LANES), BF)
            for w, _, _ in targets
        ]
        + [jax.ShapeDtypeStruct((Z * SLOTS, n), BF) for n in kept_widths],
        input_output_aliases={4 + i: o for i, (_, o) in enumerate(carried)},
        compiler_params=params(),
        name="expert",
    )(rows, wg, wu, wd, *[a for a, _ in carried])


FIRST = (((0,), (0,)), ((), ()))


def down_kernel(rep_ref, g_ref, sc_ref, keep_ref, send_ref, acc_ref):
    acc_ref[...] = lax.dot_general(sc_ref[...], g_ref[...], FIRST, preferred_element_type=F32)
    half, rep = keep_ref.shape[0], rep_ref[0]
    keep_ref[...] = acc_ref[pl.ds(pl.multiple_of(rep * half, half), half), :].astype(BF)
    send_ref[...] = acc_ref[pl.ds(pl.multiple_of((1 - rep) * half, half), half), :].astype(BF)


def gate_up_kernel(rep_ref, x_ref, dg_ref, du_ref, *outs):
    keep_g, send_g, keep_u, send_u = outs
    step, half_steps = pl.program_id(0), pl.num_programs(0) // 2
    x = x_ref[...]
    gate = lax.dot_general(x, dg_ref[...], FIRST, preferred_element_type=F32).astype(BF)
    up = lax.dot_general(x, du_ref[...], FIRST, preferred_element_type=F32).astype(BF)

    @pl.when(step < half_steps)
    def _():
        send_g[...] = gate
        send_u[...] = up

    @pl.when(step >= half_steps)
    def _():
        keep_g[...] = gate
        keep_u[...] = up


def weights_down(rep, rows, sc):
    total, hidden = sc.shape
    width = rows.shape[1] // 2
    tile = 512
    steps = width // tile
    down = pl.BlockSpec((hidden // 2, tile), lambda i, rep: (0, i))
    return pl.pallas_call(
        down_kernel,
        grid_spec=pltpu.PrefetchScalarGridSpec(
            num_scalar_prefetch=1,
            grid=(steps,),
            in_specs=[
                pl.BlockSpec((total, tile), lambda i, rep: (0, steps + i)),
                pl.BlockSpec((total, hidden), lambda i, rep: (0, 0)),
            ],
            out_specs=[down, down],
            scratch_shapes=[pltpu.VMEM((hidden, tile), F32)],
        ),
        out_shape=[jax.ShapeDtypeStruct((hidden // 2, width), BF)] * 2,
        compiler_params=params(),
        name="weights_down",
    )(rep, rows, sc)


def weights_gate_up(rep, rows, dg, du):
    total, hidden = dg.shape
    width = rows.shape[1] // 2
    tile = 512
    steps = width // tile
    half = steps // 2
    whole = pl.BlockSpec((total, hidden), lambda i, rep: (0, 0))
    keep = pl.BlockSpec((tile, hidden), lambda i, rep: (jnp.maximum(i - half, 0), 0))
    send = pl.BlockSpec((tile, hidden), lambda i, rep: (jnp.minimum(i, half - 1), 0))
    return pl.pallas_call(
        gate_up_kernel,
        grid_spec=pltpu.PrefetchScalarGridSpec(
            num_scalar_prefetch=1,
            grid=(steps,),
            in_specs=[
                pl.BlockSpec(
                    (total, tile), lambda i, rep: (0, lax.rem(i + (1 - rep[0]) * half, steps))
                ),
                whole,
                whole,
            ],
            out_specs=[keep, send, keep, send],
        ),
        out_shape=[jax.ShapeDtypeStruct((width // 2, hidden), BF)] * 4,
        compiler_params=params(),
        name="weights_gate_up",
    )(rep, rows, dg, du)


def combine_kernel(topk, count, z_ref, back_ref, *refs):
    z_me = z_ref[0].astype(F32)
    for b in range(count):
        meta = refs[b][:, 0 : 3 * LANES].astype(F32)
        out_ref = refs[count + b]
        width = out_ref.shape[1]
        hits, select = select_rows(meta, z_me, topk)
        rows = back_ref[:, b, :, 0:width].astype(F32).reshape(SLOTS, width).astype(BF)
        part = lax.dot_general(
            select, rows, (((0,), (0,)), ((), ())), preferred_element_type=F32
        )
        out_ref[0:LANES, :] = part.astype(out_ref.dtype)
        value = back_ref[:, b, :, width:].astype(F32).reshape(SLOTS, LANES)
        grads = [jnp.sum(jnp.where(h, value, 0.0), axis=0, keepdims=True) for h in hits]
        grads.append(jnp.zeros((META - topk, LANES), F32))
        grads = jnp.concatenate(grads, axis=0)
        grads = jnp.concatenate([grads, jnp.zeros((META, width - LANES), F32)], axis=1)
        out_ref[LANES : LANES + META, :] = grads.astype(out_ref.dtype)


def combine(z_me, back, blocks, topk, kinds):
    width = back.shape[-1] - LANES
    count = len(blocks)
    last = blocks[0].shape[0] // META - 1
    return pl.pallas_call(
        functools.partial(combine_kernel, topk, count),
        grid=(1,),
        in_specs=[SMEM, pl.BlockSpec(back.shape, lambda i: (0, 0, 0, 0))]
        + [pl.BlockSpec((META, width), lambda i: (last, 0))] * count,
        out_specs=[pl.BlockSpec((LANES + META, width), lambda i: (0, 0))] * count,
        out_shape=[jax.ShapeDtypeStruct((LANES + META, width), k) for k in kinds],
        compiler_params=params(),
        name="combine",
    )(z_me, back, *blocks)


def plane_exchange(value):
    return lax.all_to_all(value, PLANE, split_axis=0, concat_axis=0, tiled=True)


def body(tokens, out_grad, route, prob, w_gate, w_up, w_down):
    local, _ = tokens.shape
    topk = route.shape[1]
    wg, wu, wd = w_gate[0], w_up[0], w_down[0]
    z_me = lax.axis_index("z").reshape(1)
    rep = lax.axis_index("rep").reshape(1)

    blocks = {"a0": pack(route, prob, tokens, out_grad)}
    blocks["a1"] = z_shift(blocks["a0"], 1)
    blocks["b0"] = swap(blocks["a0"], "c")
    for s in range(1, FAR + 1):
        for kind in "ab":
            name = f"{kind}{s}"
            if name not in blocks and name != f"b{FAR}":
                blocks[name] = z_shift(blocks[f"{kind}{s - 1}"], 1)

    kept, backs = [], {}
    for group, start, targets in ROUNDS:
        sent = build(z_me, [blocks[r] for r in group], topk)
        rows = plane_exchange(sent)
        rows = rows.reshape(-1, rows.shape[-1])
        done = expert(rows, wg, wu, wd, kept, start, backs, targets)
        kept = done[len(targets) :]
        backs.update(zip((w for w, _, _ in targets), done))
    rows, sc, dg, du = kept
    halves = weights_down(rep, rows, sc)
    halves = (*weights_gate_up(rep, rows, dg, du), *halves)
    grads = []
    for name, keep, send in zip(("gate", "up", "down"), halves[0::2], halves[1::2]):
        got = swap(send, "rep")
        grads.append((keep.astype(F32) + got.astype(F32)).astype(BF)[None])

    partial = {}
    for i, group in enumerate(RETURNS):
        returned = plane_exchange(backs[i])
        kinds = [F32 if r == "a0" else BF for r in group]
        parts = combine(z_me, returned, [blocks[r] for r in group], topk, kinds)
        partial.update(zip(group, parts))
    moving = {"a": partial[f"a{FAR}"], "b": partial[f"b{FAR - 1}"]}
    for s in range(FAR - 1, -1, -1):
        for kind in "ab":
            if f"{kind}{s}" == f"b{FAR - 1}":
                continue
            came = z_shift(moving[kind], -1, cross=kind + str(s) == "b0")
            if s > 0:
                came = (partial[f"{kind}{s}"].astype(F32) + came.astype(F32)).astype(BF)
            moving[kind] = came
    ends = (partial["a0"], moving["a"], moving["b"])
    grad_tokens = sum(e[:local].astype(F32) for e in ends).astype(BF)
    grad_prob = sum(e[local : local + topk, :local].astype(F32) for e in ends).T.astype(BF)
    return (grad_tokens, grad_prob, *grads)


def solution(mesh):
    fine = Mesh(mesh.devices.reshape(-1, YH, Z, X, C), ALL)
    exp = ("yh", "z", "x", "c")
    placed = (P(ALL, None),) * 4 + (P(exp, None, None),) * 3
    return jax.shard_map(
        body,
        mesh=fine,
        in_specs=placed,
        out_specs=(P(ALL, None),) * 2 + (P(exp, "rep", None),) * 3,
        check_vma=False,
    )
```
